32 devices in a mesh: gx: 8 (over z, x), gy: 4 (over y, core).
Axes of the slice: x: 2, y: 2, z: 4, core: 2. Of those that a mesh axis runs over, the one named last changes fastest.
Arguments:
- right_side: float32 [128, 128, 128], P('gx', 'gy'), may hold values from -13 to 13
- accumulation: float32 [128, 128, 128], P('gx', 'gy'), may hold values from 0.05 to 0.5
- trans_x: float32 [128, 128, 128], P('gx', 'gy'), may hold values from 0.1 to 2
- trans_y: float32 [128, 128, 128], P('gx', 'gy'), may hold values from 0.1 to 2
- trans_z: float32 [128, 128, 128], P('gx', 'gy'), may hold values from 0.1 to 2
- perf_cells: int32 [512, 256], P(('gx', 'gy')), may hold values from 0 to 65535
- perf_live: int32 [512, 256], P(('gx', 'gy')), may hold values 0 or 1
- well_region: int32 [512, 1], P(('gx', 'gy')), may hold values from 0 to 7; in each aligned block of 16 rows (0 to 15, 16 to 31, ...) at most 2 rows name the same one
- schur_blocks: float32 [512, 256, 256], P(('gx', 'gy')), may hold values from -8 to 10, as said below
Outputs:
- pressure_update: float32 [128, 128, 128], P('gx', 'gy')
- residual: float32 [128, 128, 128], P('gx', 'gy')
The draws below stay inside these ranges and needn't reach their ends.
Inputs may be any that keep to these rules, and one draw needn't show every extreme that they name: `perf_cells`: well w is owned by the device at position w // 16 of gx+gy; its slot's cell is a flat index (x slowest, layer fastest) within the block of 16 x 32 x 128 cells of the device at x index well_region[w] and at the owner's y index. `well_region`: among the wells of one owner, no x index is named more than 2 times, and some x index exactly 2 times. `schur_blocks`: each block is symmetric positive definite.
All inputs are finite; a program needn't handle non-finite values. No bound on the sum of `perf_live` on one device may be relied on, other than what follows from the above.
Results may differ from the reference program's by a relative error of at most 0.0003.
Values sent between devices are 32-bit elements; how exact they have to be, the bound alone decides.
A program may use at most 64 MiB of HBM per device.

```python
import math
import jax
import jax.numpy as jnp
import numpy as np
from jax import lax

CX = 16
CY = 32
NZ = 128
WELL_DEV = 16
PERF = 256
WCAP = 2
ITERS = 6
NX = 128
NY = 128
WELLS = 512
N_GX = 8
N_GY = 4


def draw_right_side(key, part):
    key_noise = jax.random.fold_in(key, 11)
    pos_x = jnp.arange(NX, dtype=jnp.float32) / max(NX - 1, 1)
    pos_y = jnp.arange(NY, dtype=jnp.float32) / max(NY - 1, 1)
    scaling = jnp.exp(math.log(3.0) * (pos_x[:, None] + pos_y[None, :] - 1.0))[:, :, None]
    noise = jnp.clip(jax.random.normal(key_noise, (NX, NY, NZ), jnp.float32), -4.0, 4.0)
    return noise * scaling


def draw_schur_blocks(key, part):
    key_factor = jax.random.fold_in(key, 21)
    key_spread = jax.random.fold_in(key, 22)
    factor = jnp.clip(jax.random.normal(key_factor, (WELLS, PERF, PERF), jnp.float32), -4.0, 4.0)
    spread = jnp.exp(jax.random.uniform(key_spread, (WELLS, PERF), jnp.float32, math.log(0.5), math.log(2.0)))
    product = jnp.einsum('wik,wjk->wij', factor, factor) * (0.5 / PERF)
    eye_block = jnp.eye(PERF, dtype=jnp.float32)[None, :, :]
    return product + eye_block * spread[:, :, None]


def with_ends(array, rng, smallest, top_value):
    shape = array.shape
    spot = [jax.random.randint(jax.random.fold_in(rng, axis), (), 0, shape[axis]) for axis in range(len(shape))]
    array = array.at[tuple(spot)].set(smallest)
    longest = shape.index(max(shape))
    spot[longest] = (spot[longest] + 1) % shape[longest]
    return array.at[tuple(spot)].set(top_value)


def block_levels(stream_key, shape, split, least, top_value):
    factor_of, own = 1.0, jax.random.fold_in(stream_key, 6)
    for axis_at, blocks in split:
        steps = jnp.exp(jax.random.uniform(jax.random.fold_in(own, axis_at), (blocks,), jnp.float32, least / len(split), top_value / len(split)))
        factor_of = factor_of * jnp.repeat(steps, shape[axis_at] // blocks).reshape([-1 if axis == axis_at else 1 for axis in range(len(shape))])
    return factor_of


def assign_block(rng, own, number, rows, amount, top, most, lean):
    sequence = jax.random.permutation(rng, amount)
    heavy_load, ordinary = shares(amount, rows * top, most, lean, True), shares(amount, rows * top, most, lean, False)
    places = jnp.arange(amount)

    def named(sizes, turn):
        used = int((sizes > 0).sum())
        fixed = max(1, used // 4)
        moved = fixed + (places - fixed + turn * (used - fixed)) % max(1, amount - fixed)
        return jnp.zeros((amount,), jnp.int32).at[sequence[jnp.where(places < fixed, places, moved)]].set(jnp.asarray(sizes, jnp.int32))

    sizes = jnp.where(number % 4 == 0, named(heavy_load, number // 4), named(ordinary, number - number // 4 - 1))
    mixed = jax.random.permutation(jax.random.fold_in(own, 3), amount)
    giver, taker = mixed[0:amount // 2 * 2:2], mixed[1:amount // 2 * 2:2]
    margin = jnp.minimum(sizes[giver] - 1, most - sizes[taker]) // 2
    margin = jnp.where((giver == sequence[0]) | (taker == sequence[0]) | (sizes[taker] == 0), 0, jnp.maximum(margin, 0))
    moved = jax.random.randint(jax.random.fold_in(own, 4), (amount // 2,), 0, 1 << 20) % (margin + 1)
    sizes = sizes.at[giver].add(-moved).at[taker].add(moved)
    members = jnp.searchsorted(jnp.cumsum(sizes), jnp.arange(rows * top), side="right").astype(jnp.int32)
    table = members.reshape(top, rows).T
    table = table[jax.random.permutation(jax.random.fold_in(own, 1), rows)]
    turn = jax.random.randint(jax.random.fold_in(own, 2), (rows, 1), 0, top)
    return jnp.take_along_axis(table, (jnp.arange(top)[None, :] + turn) % top, axis=1)


def shares(amount, total, reach, lean, full):
    loads = [(1 << 20) // math.isqrt(grade ** lean) + 1 for grade in range(1, amount + 1)]
    largest = reach if full else min(reach, max(-(-total // amount), total * loads[0] // sum(loads)))
    least = 1 if total - largest >= amount - 1 else 0
    given, surplus = [largest] + [least] * (amount - 1), total - largest - least * (amount - 1)
    while surplus > 0:
        free = [i for i in range(1, amount) if given[i] < largest] or [i for i in range(1, amount) if given[i] < reach]
        mass, remaining = sum([loads[i] for i in free]), surplus
        for i in free:
            extra = min(reach - given[i], max(1, remaining * loads[i] // mass), surplus)
            given[i] = given[i] + extra
            surplus = surplus - extra
    return np.array(given)


def setup_inputs(seed: int = 0) -> dict:
    key_list = jax.random.split(jax.random.key(seed), 10)
    right_side = draw_right_side(jax.random.fold_in(key_list[9], 71), 0)
    accumulation = jnp.clip(jnp.exp(math.log(0.5) - 2.3025851 * jax.random.uniform(key_list[1], (NX, NY, NZ), jnp.float32) ** block_levels(key_list[1], (NX, NY, NZ), ((0, 8), (1, 4)), -0.2, 0.2)), 0.05, 0.5)
    trans_x = jnp.clip(jnp.exp(math.log(2.0) - 2.9957323 * jax.random.uniform(key_list[2], (NX, NY, NZ), jnp.float32) ** block_levels(key_list[2], (NX, NY, NZ), ((0, 8), (1, 4)), -0.2, 0.2)), 0.1, 2.0)
    trans_y = jnp.clip(jnp.exp(math.log(2.0) - 2.9957323 * jax.random.uniform(key_list[3], (NX, NY, NZ), jnp.float32) ** block_levels(key_list[3], (NX, NY, NZ), ((0, 8), (1, 4)), -0.2, 0.2)), 0.1, 2.0)
    trans_z = jnp.clip(jnp.exp(math.log(2.0) - 2.9957323 * jax.random.uniform(key_list[4], (NX, NY, NZ), jnp.float32) ** block_levels(key_list[4], (NX, NY, NZ), ((0, 8), (1, 4)), -0.2, 0.2)), 0.1, 2.0)
    perf_cells = with_ends(jax.random.randint(key_list[5], (WELLS, PERF), 0, CX * CY * NZ), jax.random.fold_in(key_list[5], 1), 0, (CX * CY * NZ) - 1).astype(jnp.int32)
    perf_live = with_ends((jax.random.randint(key_list[6], (WELLS, PERF), 0, 4) < 3).astype(jnp.int32), jax.random.fold_in(key_list[6], 1), 0, 1)
    well_region_keys = jax.random.split(jax.random.fold_in(key_list[7], 1), WELLS // WELL_DEV)
    well_region_turns = jax.random.permutation(jax.random.fold_in(key_list[7], 3), WELLS // WELL_DEV)
    well_region = jax.vmap(lambda own, number: assign_block(jax.random.fold_in(key_list[7], 2), own, number, WELL_DEV, N_GX, 1, WCAP, 2))(well_region_keys, well_region_turns).reshape((WELLS, 1))
    schur_blocks = draw_schur_blocks(jax.random.fold_in(key_list[9], 71), 0)
    return dict(right_side=right_side, accumulation=accumulation, trans_x=trans_x, trans_y=trans_y, trans_z=trans_z, perf_cells=perf_cells, perf_live=perf_live, well_region=well_region, schur_blocks=schur_blocks)


def shifted_prev(values, axis_number):
    widths = [(0, 0), (0, 0), (0, 0)]
    widths[axis_number] = (1, 0)
    padded = jnp.pad(values, widths)
    return lax.slice_in_dim(padded, 0, values.shape[axis_number], axis=axis_number)


def shifted_next(values, axis_number):
    widths = [(0, 0), (0, 0), (0, 0)]
    widths[axis_number] = (0, 1)
    padded = jnp.pad(values, widths)
    return lax.slice_in_dim(padded, 1, values.shape[axis_number] + 1, axis=axis_number)


def perforation_index(perf_cells, well_region):
    wells_total = perf_cells.shape[0]
    owners = jnp.arange(wells_total, dtype=jnp.int32) // WELL_DEV
    owner_y = owners % N_GY
    region = well_region[:, 0]
    layer_x = perf_cells // (CY * NZ)
    layer_y = (perf_cells // NZ) % CY
    layer_z = perf_cells % NZ
    glob_x = region[:, None] * CX + layer_x
    glob_y = owner_y[:, None] * CY + layer_y
    return ((glob_x * NY + glob_y) * NZ + layer_z).astype(jnp.int32)


def well_term(field, cell_index, live_mask, schur_blocks):
    picked = field.reshape(-1)[cell_index] * live_mask
    pushed = jnp.einsum("wij,wj->wi", schur_blocks, picked, precision=lax.Precision.HIGHEST) * live_mask
    flat = jnp.zeros((field.size,), field.dtype).at[cell_index.reshape(-1)].add(pushed.reshape(-1))
    return flat.reshape(field.shape)


def reference(right_side, accumulation, trans_x, trans_y, trans_z, perf_cells, perf_live, well_region, schur_blocks):
    face_x = trans_x.at[-1].set(0.0)
    face_y = trans_y.at[:, -1].set(0.0)
    face_z = trans_z.at[:, :, -1].set(0.0)
    prev_x = shifted_prev(face_x, 0)
    prev_y = shifted_prev(face_y, 1)
    prev_z = shifted_prev(face_z, 2)
    diagonal = accumulation + face_x + prev_x + face_y + prev_y + face_z + prev_z
    cell_index = perforation_index(perf_cells, well_region)
    live_mask = perf_live.astype(right_side.dtype)

    def operate(field):
        local_part = (accumulation * field
                      + face_x * (field - shifted_next(field, 0)) + prev_x * (field - shifted_prev(field, 0))
                      + face_y * (field - shifted_next(field, 1)) + prev_y * (field - shifted_prev(field, 1))
                      + face_z * (field - shifted_next(field, 2)) + prev_z * (field - shifted_prev(field, 2)))
        return local_part + well_term(field, cell_index, live_mask, schur_blocks)

    solution = jnp.zeros_like(right_side)
    residual = right_side
    precon = residual / diagonal
    direction = precon
    product_now = jnp.sum(residual * precon)
    for counter in range(ITERS):
        applied = operate(direction)
        step_size = product_now / jnp.sum(direction * applied)
        solution = solution + step_size * direction
        residual = residual - step_size * applied
        precon = residual / diagonal
        product_next = jnp.sum(residual * precon)
        direction = precon + (product_next / product_now) * direction
        product_now = product_next
    return solution, residual
```

```python
import functools

import jax
import jax.numpy as jnp
from jax import lax
from jax.experimental import pallas as pl
from jax.experimental.pallas import tpu as pltpu
from jax.sharding import PartitionSpec as P

WCAP = 2
ITERS = 6
ROWS = 4
MESH = pl.DeviceIdType.MESH


def split_bf16(values):
    high = values.astype(jnp.bfloat16).astype(jnp.float32)
    return high, values - high


def kernel(
    n,
    ny,
    rows_x,
    rows_y,
    region_ref,
    rhs_ref,
    acc_ref,
    tx_ref,
    ty_ref,
    tz_ref,
    cells_ref,
    live_ref,
    schur_hbm,
    x_ref,
    r_ref,
    schur_vm,
    schur_two,
    onehot,
    vl_ref,
    lay_ref,
    live_slot,
    req_send,
    req_recv,
    send_b,
    recv_b,
    send_c,
    recv_c,
    send_g,
    recv_g,
    ysend,
    xrecv,
    yrecv,
    yface_send,
    xface_recv,
    yface_recv,
    fx_ref,
    fy_ref,
    py_ref,
    fz_ref,
    pz_ref,
    inv_ref,
    m_ref,
    w_ref,
    z_ref,
    p_ref,
    s_ref,
    nloc_ref,
    dots_ref,
    local_sem,
    req_ss,
    req_rs,
    face_ss,
    face_rs,
    halo_ss,
    halo_rs,
    b_ss,
    b_rs,
    c_ss,
    c_rs,
    g_ss,
    g_rs,
):
    cols, layers = rhs_ref.shape
    wells, perf = cells_ref.shape
    chunk = WCAP * perf
    shift = layers.bit_length() - 1
    assert layers == 1 << shift
    me, my = lax.axis_index("gx"), lax.axis_index("gy")

    def at_x(d):
        return {"gx": lax.rem(me + (d + n), n)}

    def at_y(d):
        return {"gy": lax.rem(my + (d + ny), ny)}

    def remote(src, dst, ss, rs, where):
        return pltpu.make_async_remote_copy(
            src_ref=src, dst_ref=dst, send_sem=ss, recv_sem=rs, device_id=where, device_id_type=MESH
        )

    schur_copy = pltpu.make_async_copy(schur_hbm, schur_vm, local_sem)
    schur_copy.start()
    barrier = pltpu.get_barrier_semaphore()
    for d in range(1, n):
        pl.semaphore_signal(barrier, inc=1, device_id=at_x(d), device_id_type=MESH)
    for d in range(1, ny):
        pl.semaphore_signal(barrier, inc=1, device_id=at_y(d), device_id_type=MESH)

    well_at = []
    for d in range(n):
        peer = lax.rem(me + d, n)
        found = [jnp.int32(0)] * WCAP
        count = jnp.int32(0)
        for w in range(wells):
            match = region_ref[w, 0] == peer
            for j in range(WCAP):
                found[j] = jnp.where(jnp.logical_and(match, count == j), jnp.int32(w), found[j])
            count = count + match.astype(jnp.int32)
        well_at.append(found)
        for j in range(WCAP):
            used = (count > j).astype(jnp.int32)
            cells = cells_ref[pl.ds(found[j], 1), :] * used
            live = live_ref[pl.ds(found[j], 1), :] * used
            target = req_send if d else req_recv
            target[d, j : j + 1, :] = cells
            live_slot[d, j : j + 1, :] = live.astype(jnp.float32)
    yface_send[...] = ty_ref[pl.ds(rows_y - 1, rows_x, stride=rows_y), :]

    pl.semaphore_wait(barrier, n - 1 + ny - 1)
    req_out = [
        remote(req_send.at[d], req_recv.at[n - d], req_ss.at[d], req_rs.at[n - d], at_x(d))
        for d in range(1, n)
    ]
    req_in = [
        remote(req_send.at[d], req_recv.at[d], req_ss.at[d], req_rs.at[d], at_x(d)) for d in range(1, n)
    ]
    face_out = [
        remote(
            tx_ref.at[pl.ds(cols - rows_y, rows_y)], xface_recv, face_ss.at[0], face_rs.at[0], at_x(1)
        ),
        remote(yface_send, yface_recv, face_ss.at[1], face_rs.at[1], at_y(1)),
    ]
    for copy in req_out + face_out:
        copy.start()

    last_x = me == n - 1
    last_y = my == ny - 1
    lane = lax.broadcasted_iota(jnp.int32, (rows_y, layers), 1)
    row = lax.broadcasted_iota(jnp.int32, (rows_y, layers), 0)
    zeros = jnp.zeros((rows_y, layers), jnp.float32)
    for copy in face_out:
        copy.wait()
    fx_ref[0:rows_y, :] = jnp.where(me == 0, 0.0, xface_recv[...])
    gamma = jnp.zeros((8, layers), jnp.float32)
    for i in range(rows_x):
        at = slice(i * rows_y, (i + 1) * rows_y)
        after = slice((i + 1) * rows_y, (i + 2) * rows_y)
        fx = tx_ref[at, :]
        if i == rows_x - 1:
            fx = jnp.where(last_x, 0.0, fx)
        fx_ref[after, :] = fx
        fy = ty_ref[at, :]
        below = jnp.where(my == 0, 0.0, yface_recv[i : i + 1, :])
        py = jnp.where(row == 0, below, pltpu.roll(fy, 1, 0))
        fy = jnp.where(jnp.logical_and(last_y, row == rows_y - 1), 0.0, fy)
        fy_ref[at, :] = fy
        py_ref[at, :] = py
        fz = jnp.where(lane == layers - 1, 0.0, tz_ref[at, :])
        pz = pltpu.roll(fz, 1, 1)
        fz_ref[at, :] = fz
        pz_ref[at, :] = pz
        diagonal = acc_ref[at, :] + fx + fx_ref[at, :] + fy + py + fz + pz
        inverse = 1.0 / diagonal
        inv_ref[at, :] = inverse
        r = rhs_ref[at, :]
        r_ref[at, :] = r
        u = r * inverse
        m_ref[at, :] = u
        for ref in (x_ref, w_ref, z_ref, p_ref, s_ref):
            ref[at, :] = zeros
    dots_ref[...] = jnp.zeros_like(dots_ref)

    column = lax.broadcasted_iota(jnp.int32, (cols, chunk), 0)
    for d in range(n):
        if d:
            req_in[d - 1].wait_recv()
        cells = jnp.concatenate([req_recv[d, j : j + 1, :] for j in range(WCAP)], 1)
        lay_ref[d] = jnp.bitwise_and(cells, layers - 1)
        onehot[:, d * chunk : (d + 1) * chunk] = (
            (column == lax.shift_right_logical(cells, shift)).astype(jnp.float32).astype(jnp.bfloat16)
        )
    for copy in req_out:
        copy.wait_send()

    schur_copy.wait()
    for d in range(n):
        for j in range(WCAP):
            slot = d * WCAP + j
            block = schur_vm[well_at[d][j]]
            high = block.astype(jnp.bfloat16)
            schur_two[slot, 0:perf, :] = high
            schur_two[slot, perf : 2 * perf, :] = (block - high.astype(jnp.float32)).astype(jnp.bfloat16)

    layer = lax.broadcasted_iota(jnp.int32, (layers, chunk), 0)
    pick_row = lax.broadcasted_iota(jnp.int32, (16, perf), 0)

    def b_copy(par, d, slot):
        return remote(send_b.at[par, d], recv_b.at[par, slot], b_ss.at[par, d], b_rs.at[par, slot], at_x(d))

    def c_copy(par, d, slot):
        return remote(send_c.at[par, d], recv_c.at[par, slot], c_ss.at[par, d], c_rs.at[par, slot], at_x(d))

    def g_copy(par, d, slot):
        return remote(send_g.at[par], recv_g.at[par, slot], g_ss.at[par, d], g_rs.at[par, slot], at_y(d))

    def halo_copies(par):
        return [
            remote(
                m_ref.at[pl.ds(cols - rows_y, rows_y)],
                xrecv.at[par, 0],
                halo_ss.at[par, 0],
                halo_rs.at[par, 0],
                at_x(1),
            ),
            remote(
                m_ref.at[pl.ds(0, rows_y)], xrecv.at[par, 1], halo_ss.at[par, 1], halo_rs.at[par, 1], at_x(-1)
            ),
            remote(ysend.at[par, 0], yrecv.at[par, 0], halo_ss.at[par, 2], halo_rs.at[par, 2], at_y(1)),
            remote(ysend.at[par, 1], yrecv.at[par, 1], halo_ss.at[par, 3], halo_rs.at[par, 3], at_y(-1)),
        ]

    def start_sums(par):
        total = recv_b[par, 0, 2:3, :]
        for d in range(1, n):
            total = total + recv_b[par, d, 2:3, :]
        send_g[par] = total
        for d in range(1, ny):
            g_copy(par, d, ny - d).start()
        return total

    def end_sums(par, total):
        for d in range(1, ny):
            g_copy(par, d, d).wait_recv()
            total = total + recv_g[par, d]
        for d in range(1, ny):
            g_copy(par, d, d).wait_send()
        gam = jnp.sum(total[:, :layers], axis=1, keepdims=True)
        dlt = jnp.sum(total[:, layers:], axis=1, keepdims=True)
        return jnp.broadcast_to(gam, (1, layers)), jnp.broadcast_to(dlt, (1, layers))

    def step(k, carried):
        gam_old, a_old = carried
        par = lax.rem(k, 2)
        ysend[par, 0] = m_ref[pl.ds(rows_y - 1, rows_x, stride=rows_y), :]
        ysend[par, 1] = m_ref[pl.ds(0, rows_x, stride=rows_y), :]
        halos = halo_copies(par)
        for copy in halos:
            copy.start()

        turned = m_ref[...].T
        high, low = split_bf16(turned)
        lhs = jnp.concatenate([high, low], 0).astype(jnp.bfloat16)
        dots = dots_ref[...]
        for d in list(range(1, n)) + [0]:
            part = jnp.dot(
                lhs, onehot[:, d * chunk : (d + 1) * chunk], preferred_element_type=jnp.float32
            )
            part = part[:layers] + part[layers:]
            picked = jnp.sum(jnp.where(layer == lay_ref[d], part, 0.0), axis=0, keepdims=True)
            target = send_b if d else recv_b
            for j in range(WCAP):
                target[par, d, j : j + 1, :] = picked[:, j * perf : (j + 1) * perf]
            target[par, d, 2:3, :] = dots
            if d:
                b_copy(par, d, n - d).start()

        for copy in halos:
            copy.wait()
        for i in range(rows_x):
            at = slice(i * rows_y, (i + 1) * rows_y)
            after = slice((i + 1) * rows_y, (i + 2) * rows_y)
            m = m_ref[at, :]
            below = m_ref[(i - 1) * rows_y : i * rows_y, :] if i else xrecv[par, 0]
            above = m_ref[after, :] if i < rows_x - 1 else xrecv[par, 1]
            y_prev = jnp.where(row == 0, yrecv[par, 0, i : i + 1, :], pltpu.roll(m, 1, 0))
            y_next = jnp.where(row == rows_y - 1, yrecv[par, 1, i : i + 1, :], pltpu.roll(m, rows_y - 1, 0))
            nloc_ref[at, :] = (
                acc_ref[at, :] * m
                + fx_ref[after, :] * (m - above)
                + fx_ref[at, :] * (m - below)
                + fy_ref[at, :] * (m - y_next)
                + py_ref[at, :] * (m - y_prev)
                + fz_ref[at, :] * (m - pltpu.roll(m, layers - 1, 1))
                + pz_ref[at, :] * (m - pltpu.roll(m, 1, 1))
            )

        for d in range(n):
            if d:
                b_copy(par, d, d).wait_recv()
            target = send_c if d else recv_c
            for j in range(WCAP):
                live = live_slot[d, j : j + 1, :]
                high, low = split_bf16(recv_b[par, d, j : j + 1, :] * live)
                left = jnp.where(pick_row == 0, high, jnp.where(pick_row == 1, low, 0.0)).astype(jnp.bfloat16)
                pushed = jnp.dot(
                    jnp.concatenate([left, left], 1),
                    schur_two[d * WCAP + j],
                    preferred_element_type=jnp.float32,
                )
                target[par, d, j : j + 1, :] = jnp.sum(pushed, axis=0, keepdims=True) * live
            if d:
                c_copy(par, d, n - d).start()
        total = start_sums(par)
        gam, dlt = end_sums(par, total)
        b = jnp.where(k <= 1, 0.0, gam / gam_old)
        a = jnp.where(k == 0, 0.0, jnp.where(k == 1, gam / dlt, gam / (dlt - b * gam / a_old)))
        a_w = jnp.where(k == 0, -1.0, a)
        gamma = jnp.zeros((8, layers), jnp.float32)
        for i in range(rows_x):
            at = slice(i * rows_y, (i + 1) * rows_y)
            inverse = inv_ref[at, :]
            r = r_ref[at, :]
            p = r * inverse + b * p_ref[at, :]
            s = w_ref[at, :] + b * s_ref[at, :]
            p_ref[at, :] = p
            s_ref[at, :] = s
            x_ref[at, :] = x_ref[at, :] + a * p
            r = r - a * s
            r_ref[at, :] = r
            gamma = gamma + jnp.sum((r * r * inverse).reshape(rows_y // 8, 8, layers), axis=0)

        for d in range(n):
            if d:
                c_copy(par, d, d).wait_recv()
            back = jnp.concatenate([recv_c[par, d, j : j + 1, :] for j in range(WCAP)], 1)
            high, low = split_bf16(back)
            here = layer == lay_ref[d]
            span = slice(d * chunk, (d + 1) * chunk)
            vl_ref[0:layers, span] = jnp.where(here, high, 0.0).astype(jnp.bfloat16)
            vl_ref[layers : 2 * layers, span] = jnp.where(here, low, 0.0).astype(jnp.bfloat16)
        wide = lax.dot_general(
            onehot[...], vl_ref[...], (((1,), (1,)), ((), ())), preferred_element_type=jnp.float32
        )
        spread = wide[:, :layers] + wide[:, layers:]
        delta = jnp.zeros((8, layers), jnp.float32)
        for i in range(rows_x):
            at = slice(i * rows_y, (i + 1) * rows_y)
            z = nloc_ref[at, :] + spread[at, :] + b * z_ref[at, :]
            z_ref[at, :] = z
            w = w_ref[at, :] - a_w * z
            w_ref[at, :] = w
            m = w * inv_ref[at, :]
            m_ref[at, :] = m
            delta = delta + jnp.sum((m * r_ref[at, :]).reshape(rows_y // 8, 8, layers), axis=0)
        dots_ref[:, :layers] = jnp.sum(gamma, axis=0, keepdims=True)
        dots_ref[:, layers:] = jnp.sum(delta, axis=0, keepdims=True)
        for d in range(1, n):
            b_copy(par, d, d).wait_send()
            c_copy(par, d, d).wait_send()
        return gam, a

    ones = jnp.ones((1, layers), jnp.float32)
    gam_old, a_old = lax.fori_loop(0, ITERS, step, (ones, ones))

    par = ITERS % 2
    recv_b[par, 0, 2:3, :] = dots_ref[...]
    for d in range(1, n):
        send_b[par, d, 2:3, :] = dots_ref[...]
        b_copy(par, d, n - d).start()
    for d in range(1, n):
        b_copy(par, d, d).wait_recv()
    total = start_sums(par)
    for d in range(1, n):
        b_copy(par, d, d).wait_send()
    gam, dlt = end_sums(par, total)
    b = gam / gam_old
    a = gam / (dlt - b * gam / a_old)
    for i in range(rows_x):
        at = slice(i * rows_y, (i + 1) * rows_y)
        r = r_ref[at, :]
        p = r * inv_ref[at, :] + b * p_ref[at, :]
        s = w_ref[at, :] + b * s_ref[at, :]
        x_ref[at, :] = x_ref[at, :] + a * p
        r_ref[at, :] = r - a * s


def local(
    right_side,
    accumulation,
    trans_x,
    trans_y,
    trans_z,
    perf_cells,
    perf_live,
    well_region,
    schur_blocks,
):
    rows_x, rows_y, layers = right_side.shape
    cols = rows_x * rows_y
    wells, perf = perf_cells.shape
    n, ny = lax.axis_size("gx"), lax.axis_size("gy")
    chunk = WCAP * perf
    f32, bf16, i32 = jnp.float32, jnp.bfloat16, jnp.int32
    vmem, dma = pltpu.VMEM, pltpu.SemaphoreType.DMA
    field = vmem((cols, layers), f32)
    fields = [value.reshape(cols, layers) for value in (right_side, accumulation, trans_x, trans_y, trans_z)]
    in_vmem = pl.BlockSpec(memory_space=pltpu.VMEM)
    outs = pl.pallas_call(
        functools.partial(kernel, n, ny, rows_x, rows_y),
        out_shape=[jax.ShapeDtypeStruct((cols, layers), f32)] * 2,
        in_specs=[pl.BlockSpec(memory_space=pltpu.SMEM)]
        + [in_vmem] * 7
        + [pl.BlockSpec(memory_space=pl.ANY)],
        out_specs=[in_vmem] * 2,
        scratch_shapes=[
            vmem((wells, perf, perf), f32),
            vmem((n * WCAP, 2 * perf, perf), bf16),
            vmem((cols, n * chunk), bf16),
            vmem((2 * layers, n * chunk), bf16),
            vmem((n, 1, chunk), i32),
            vmem((n, WCAP, perf), f32),
            vmem((n, WCAP, perf), i32),
            vmem((n, WCAP, perf), i32),
            vmem((2, n, ROWS, 2 * layers), f32),
            vmem((2, n, ROWS, 2 * layers), f32),
            vmem((2, n, WCAP, perf), f32),
            vmem((2, n, WCAP, perf), f32),
            vmem((2, 1, 2 * layers), f32),
            vmem((2, ny, 1, 2 * layers), f32),
            vmem((2, 2, rows_x, layers), f32),
            vmem((2, 2, rows_y, layers), f32),
            vmem((2, 2, rows_x, layers), f32),
            vmem((rows_x, layers), f32),
            vmem((rows_y, layers), f32),
            vmem((rows_x, layers), f32),
            vmem((cols + rows_y, layers), f32),
        ]
        + [field] * 11
        + [
            vmem((1, 2 * layers), f32),
            dma,
            dma((n,)),
            dma((n,)),
            dma((2,)),
            dma((2,)),
            dma((2, 4)),
            dma((2, 4)),
            dma((2, n)),
            dma((2, n)),
            dma((2, n)),
            dma((2, n)),
            dma((2, ny)),
            dma((2, ny)),
        ],
        compiler_params=pltpu.CompilerParams(
            collective_id=0, has_side_effects=True, vmem_limit_bytes=60 * 1024 * 1024
        ),
    )(well_region, *fields, perf_cells, perf_live, schur_blocks)
    return tuple(value.reshape(right_side.shape) for value in outs)


def solution(mesh):
    field, rows = P("gx", "gy", None), P(("gx", "gy"), None)
    return jax.shard_map(
        local,
        mesh=mesh,
        in_specs=(field,) * 5 + (rows,) * 3 + (P(("gx", "gy"), None, None),),
        out_specs=(field, field),
        check_vma=False,
    )
```

```python
import functools

import jax
import jax.numpy as jnp
from jax import lax
from jax.experimental import pallas as pl
from jax.experimental.pallas import tpu as pltpu
from jax.sharding import PartitionSpec as P

WCAP = 2
ITERS = 6
GROUPS = (6, 8)
EARLY = 6
MESH = pl.DeviceIdType.MESH


def split_bf16(values):
    high = values.astype(jnp.bfloat16).astype(jnp.float32)
    return high, values - high


def kernel(
    n,
    ny,
    rows_x,
    rows_y,
    region_ref,
    rhs_hbm,
    acc_hbm,
    tx_hbm,
    ty_hbm,
    tz_hbm,
    cells_ref,
    live_ref,
    schur_hbm,
    x_ref,
    r_ref,
    rhs_ref,
    acc_ref,
    tx_ref,
    ty_ref,
    tz_ref,
    schur_vm,
    schur_two,
    onehot,
    vl_ref,
    lay_ref,
    live_slot,
    req_send,
    req_recv,
    send_b,
    recv_b,
    send_c,
    recv_c,
    send_g,
    recv_g,
    ysend,
    xrecv,
    yrecv,
    yface_send,
    xface_recv,
    yface_recv,
    fx_ref,
    fy_ref,
    py_ref,
    fz_ref,
    pz_ref,
    inv_ref,
    m_ref,
    w_ref,
    z_ref,
    p_ref,
    s_ref,
    nloc_ref,
    dots_ref,
    local_sem,
    field_sem,
    req_ss,
    req_rs,
    face_ss,
    face_rs,
    halo_ss,
    halo_rs,
    b_ss,
    b_rs,
    c_ss,
    c_rs,
    g_ss,
    g_rs,
):
    cols, layers = rhs_ref.shape
    wells, perf = cells_ref.shape
    chunk = WCAP * perf
    shift = layers.bit_length() - 1
    assert layers == 1 << shift and n == 1 << (n.bit_length() - 1)
    me, my = lax.axis_index("gx"), lax.axis_index("gy")

    def across(d):
        peer = me
        for bit in range(n.bit_length() - 1):
            if d >> bit & 1:
                peer = peer + (1 << bit) * (1 - 2 * lax.rem(lax.div(me, 1 << bit), 2))
        return peer

    def at_peer(d):
        return {"gx": across(d)}

    def at_x(d):
        return {"gx": lax.rem(me + (d + n), n)}

    def at_y(d):
        return {"gy": lax.rem(my + (d + ny), ny)}

    def remote(src, dst, ss, rs, where):
        return pltpu.make_async_remote_copy(
            src_ref=src, dst_ref=dst, send_sem=ss, recv_sem=rs, device_id=where, device_id_type=MESH
        )

    schur_copy = pltpu.make_async_copy(schur_hbm, schur_vm, local_sem)
    loads = [
        pltpu.make_async_copy(src, dst, field_sem.at[i])
        for i, (src, dst) in enumerate(
            (
                (ty_hbm, ty_ref),
                (tx_hbm, tx_ref),
                (tz_hbm, tz_ref),
                (acc_hbm, acc_ref),
                (rhs_hbm, rhs_ref),
            )
        )
    ]
    for copy in loads:
        copy.start()
    schur_copy.start()
    xrecv[...] = jnp.zeros_like(xrecv)
    barrier = pltpu.get_barrier_semaphore()
    for d in range(1, n):
        pl.semaphore_signal(barrier, inc=1, device_id=at_peer(d), device_id_type=MESH)
    for d in range(1, ny):
        pl.semaphore_signal(barrier, inc=1, device_id=at_y(d), device_id_type=MESH)

    well_at = []
    for d in range(n):
        peer = across(d)
        found = [jnp.int32(0)] * WCAP
        count = jnp.int32(0)
        for w in range(wells):
            match = region_ref[0, w] == peer
            for j in range(WCAP):
                found[j] = jnp.where(jnp.logical_and(match, count == j), jnp.int32(w), found[j])
            count = count + match.astype(jnp.int32)
        well_at.append(found)
        target = req_send if d else req_recv
        for j in range(WCAP):
            used = (count > j).astype(jnp.int32)
            span = slice(j * perf, (j + 1) * perf)
            target[d, :, span] = cells_ref[pl.ds(found[j], 1), :] * used
            live_slot[d, :, span] = (live_ref[pl.ds(found[j], 1), :] * used).astype(jnp.float32)
    loads[0].wait()
    loads[1].wait()
    yface_send[...] = ty_ref[pl.ds(rows_y - 1, rows_x, stride=rows_y), :]

    pl.semaphore_wait(barrier, n - 1 + ny - 1)
    requests = [
        remote(req_send.at[d], req_recv.at[d], req_ss.at[d], req_rs.at[d], at_peer(d)) for d in range(1, n)
    ]
    face_out = [
        remote(
            tx_ref.at[pl.ds(cols - rows_y, rows_y)], xface_recv, face_ss.at[0], face_rs.at[0], at_x(1)
        ),
        remote(yface_send, yface_recv, face_ss.at[1], face_rs.at[1], at_y(1)),
    ]
    for copy in requests[::-1] + face_out:
        copy.start()

    schur_copy.wait()
    for d in range(n):
        for j in range(WCAP):
            slot = d * WCAP + j
            block = schur_vm[well_at[d][j]]
            high = block.astype(jnp.bfloat16)
            schur_two[slot, 0:perf, :] = high
            schur_two[slot, perf : 2 * perf, :] = (block - high.astype(jnp.float32)).astype(jnp.bfloat16)

    last_x = me == n - 1
    last_y = my == ny - 1
    lane = lax.broadcasted_iota(jnp.int32, (rows_y, layers), 1)
    row = lax.broadcasted_iota(jnp.int32, (rows_y, layers), 0)
    zeros = jnp.zeros((rows_y, layers), jnp.float32)
    for copy in loads[2:]:
        copy.wait()
    for copy in face_out:
        copy.wait()
    fx_ref[0:rows_y, :] = jnp.where(me == 0, 0.0, xface_recv[...])
    for i in range(rows_x):
        at = slice(i * rows_y, (i + 1) * rows_y)
        after = slice((i + 1) * rows_y, (i + 2) * rows_y)
        fx = tx_ref[at, :]
        if i == rows_x - 1:
            fx = jnp.where(last_x, 0.0, fx)
        fx_ref[after, :] = fx
        fy = ty_ref[at, :]
        below = jnp.where(my == 0, 0.0, yface_recv[i : i + 1, :])
        py = jnp.where(row == 0, below, pltpu.roll(fy, 1, 0))
        fy = jnp.where(jnp.logical_and(last_y, row == rows_y - 1), 0.0, fy)
        fy_ref[at, :] = fy
        py_ref[at, :] = py
        fz = jnp.where(lane == layers - 1, 0.0, tz_ref[at, :])
        pz = pltpu.roll(fz, 1, 1)
        fz_ref[at, :] = fz
        pz_ref[at, :] = pz
        diagonal = acc_ref[at, :] + fx + fx_ref[at, :] + fy + py + fz + pz
        inverse = 1.0 / diagonal
        inv_ref[at, :] = inverse
        r = rhs_ref[at, :]
        r_ref[at, :] = r
        u = r * inverse
        m_ref[at, :] = u
        for ref in (x_ref, w_ref, z_ref, p_ref, s_ref):
            ref[at, :] = zeros
    dots_ref[...] = jnp.zeros_like(dots_ref)

    column = lax.broadcasted_iota(jnp.int32, (cols, chunk), 0)
    for d in range(n):
        if d:
            requests[d - 1].wait_recv()
        cells = req_recv[d]
        lay_ref[d] = jnp.bitwise_and(cells, layers - 1)
        onehot[:, d * chunk : (d + 1) * chunk] = (
            (column == lax.shift_right_logical(cells, shift)).astype(jnp.float32).astype(jnp.bfloat16)
        )
    for copy in requests:
        copy.wait_send()

    layer = lax.broadcasted_iota(jnp.int32, (layers, chunk), 0)
    pick_row = lax.broadcasted_iota(jnp.int32, (16, perf), 0)

    half = layers // 2
    first_half = lax.broadcasted_iota(jnp.int32, (1, layers), 1) < half

    def b_copy(par, d):
        return remote(send_b.at[par, d], recv_b.at[par, d], b_ss.at[par, d], b_rs.at[par, d], at_peer(d))

    def c_copy(par, d):
        return remote(send_c.at[par, d], recv_c.at[par, d], c_ss.at[par, d], c_rs.at[par, d], at_peer(d))

    def g_copy(par, d, slot):
        return remote(send_g.at[par], recv_g.at[par, slot], g_ss.at[par, d], g_rs.at[par, slot], at_y(d))

    def halo_copies(par):
        return [
            remote(
                m_ref.at[pl.ds(cols - rows_y, rows_y)],
                xrecv.at[par, 0],
                halo_ss.at[par, 0],
                halo_rs.at[par, 0],
                at_x(1),
            ),
            remote(
                m_ref.at[pl.ds(0, rows_y)], xrecv.at[par, 1], halo_ss.at[par, 1], halo_rs.at[par, 1], at_x(-1)
            ),
            remote(ysend.at[par, 0], yrecv.at[par, 0], halo_ss.at[par, 2], halo_rs.at[par, 2], at_y(1)),
            remote(ysend.at[par, 1], yrecv.at[par, 1], halo_ss.at[par, 3], halo_rs.at[par, 3], at_y(-1)),
        ]

    def start_sums(par):
        total = recv_b[par, 0, :, chunk:]
        for d in range(1, n):
            total = total + recv_b[par, d, :, chunk:]
        send_g[par] = total
        for d in range(1, ny):
            g_copy(par, d, ny - d).start()
        return total

    def end_sums(par, total):
        for d in range(1, ny):
            g_copy(par, d, d).wait_recv()
            total = total + recv_g[par, d]
        for d in range(1, ny):
            g_copy(par, d, d).wait_send()
        gam = jnp.sum(jnp.where(first_half, total, 0.0), axis=1, keepdims=True)
        dlt = jnp.sum(jnp.where(first_half, 0.0, total), axis=1, keepdims=True)
        return jnp.broadcast_to(gam, (1, layers)), jnp.broadcast_to(dlt, (1, layers))

    def step(k, carried):
        gam_old, a_old = carried
        par = lax.rem(k, 2)
        ysend[par, 0] = m_ref[pl.ds(rows_y - 1, rows_x, stride=rows_y), :]
        ysend[par, 1] = m_ref[pl.ds(0, rows_x, stride=rows_y), :]
        halos = halo_copies(par)
        x_up, x_down = halos[:2]
        pl.when(me < n - 1)(x_up.start)
        pl.when(me > 0)(x_down.start)
        for copy in halos[2:]:
            copy.start()

        turned = m_ref[...].T
        high, low = split_bf16(turned)
        lhs = jnp.concatenate([high, low], 0).astype(jnp.bfloat16)
        dots = dots_ref[...]
        for d in range(n - 1, -1, -1):
            part = jnp.dot(
                lhs, onehot[:, d * chunk : (d + 1) * chunk], preferred_element_type=jnp.float32
            )
            part = part[:layers] + part[layers:]
            picked = jnp.sum(jnp.where(layer == lay_ref[d], part, 0.0), axis=0, keepdims=True)
            target = send_b if d else recv_b
            target[par, d, :, :chunk] = picked
            target[par, d, :, chunk:] = dots
            if d:
                b_copy(par, d).start()

        def push(d):
            if d:
                b_copy(par, d).wait_recv()
            target = send_c if d else recv_c
            for j in range(WCAP):
                span = slice(j * perf, (j + 1) * perf)
                live = live_slot[d, :, span]
                high, low = split_bf16(recv_b[par, d, :, span] * live)
                left = jnp.where(pick_row == 0, high, jnp.where(pick_row == 1, low, 0.0)).astype(jnp.bfloat16)
                pushed = jnp.dot(
                    jnp.concatenate([left, left], 1),
                    schur_two[d * WCAP + j],
                    preferred_element_type=jnp.float32,
                )
                target[par, d, :, span] = jnp.sum(pushed, axis=0, keepdims=True) * live
            if d:
                c_copy(par, d).start()

        for d in range(EARLY):
            push(d)
        @pl.when(me < n - 1)
        def _():
            x_up.wait_send()
            x_down.wait_recv()

        @pl.when(me > 0)
        def _():
            x_up.wait_recv()
            x_down.wait_send()

        for copy in halos[2:]:
            copy.wait()
        for i in range(rows_x):
            at = slice(i * rows_y, (i + 1) * rows_y)
            after = slice((i + 1) * rows_y, (i + 2) * rows_y)
            m = m_ref[at, :]
            below = m_ref[(i - 1) * rows_y : i * rows_y, :] if i else xrecv[par, 0]
            above = m_ref[after, :] if i < rows_x - 1 else xrecv[par, 1]
            y_prev = jnp.where(row == 0, yrecv[par, 0, i : i + 1, :], pltpu.roll(m, 1, 0))
            y_next = jnp.where(row == rows_y - 1, yrecv[par, 1, i : i + 1, :], pltpu.roll(m, rows_y - 1, 0))
            nloc_ref[at, :] = (
                acc_ref[at, :] * m
                + fx_ref[after, :] * (m - above)
                + fx_ref[at, :] * (m - below)
                + fy_ref[at, :] * (m - y_next)
                + py_ref[at, :] * (m - y_prev)
                + fz_ref[at, :] * (m - pltpu.roll(m, layers - 1, 1))
                + pz_ref[at, :] * (m - pltpu.roll(m, 1, 1))
            )
        for d in range(EARLY, n):
            push(d)
        total = start_sums(par)
        gam, dlt = end_sums(par, total)
        b = jnp.where(k <= 1, 0.0, gam / gam_old)
        a = jnp.where(k == 0, 0.0, jnp.where(k == 1, gam / dlt, gam / (dlt - b * gam / a_old)))
        a_w = jnp.where(k == 0, -1.0, a)
        gamma = jnp.zeros((8, layers), jnp.float32)
        for i in range(rows_x):
            at = slice(i * rows_y, (i + 1) * rows_y)
            inverse = inv_ref[at, :]
            r = r_ref[at, :]
            p = r * inverse + b * p_ref[at, :]
            s = w_ref[at, :] + b * s_ref[at, :]
            p_ref[at, :] = p
            s_ref[at, :] = s
            x_ref[at, :] = x_ref[at, :] + a * p
            r = r - a * s
            r_ref[at, :] = r
            gamma = gamma + jnp.sum((r * r * inverse).reshape(rows_y // 8, 8, layers), axis=0)

        ends = [n * part // 8 for part in GROUPS]
        for first, end in zip([0] + ends[:-1], ends):
            for d in range(first, end):
                if d:
                    c_copy(par, d).wait_recv()
                high, low = split_bf16(recv_c[par, d])
                here = layer == lay_ref[d]
                span = slice(d * chunk, (d + 1) * chunk)
                vl_ref[0:layers, span] = jnp.where(here, high, 0.0).astype(jnp.bfloat16)
                vl_ref[layers : 2 * layers, span] = jnp.where(here, low, 0.0).astype(jnp.bfloat16)
            span = slice(first * chunk, end * chunk)
            wide = lax.dot_general(
                onehot[:, span],
                vl_ref[:, span],
                (((1,), (1,)), ((), ())),
                preferred_element_type=jnp.float32,
            )
            if end < n:
                nloc_ref[...] += wide[:, :layers] + wide[:, layers:]
        delta = jnp.zeros((8, layers), jnp.float32)
        for i in range(rows_x):
            at = slice(i * rows_y, (i + 1) * rows_y)
            z = nloc_ref[at, :] + (wide[at, :layers] + wide[at, layers:]) + b * z_ref[at, :]
            z_ref[at, :] = z
            w = w_ref[at, :] - a_w * z
            w_ref[at, :] = w
            m = w * inv_ref[at, :]
            m_ref[at, :] = m
            delta = delta + jnp.sum((m * r_ref[at, :]).reshape(rows_y // 8, 8, layers), axis=0)
        gamma = jnp.sum(gamma, axis=0, keepdims=True)
        delta = jnp.sum(delta, axis=0, keepdims=True)
        dots_ref[...] = jnp.where(
            first_half, gamma + pltpu.roll(gamma, half, 1), delta + pltpu.roll(delta, half, 1)
        )
        for d in range(1, n):
            b_copy(par, d).wait_send()
            c_copy(par, d).wait_send()
        return gam, a

    ones = jnp.ones((1, layers), jnp.float32)
    gam_old, a_old = lax.fori_loop(0, ITERS, step, (ones, ones))

    par = ITERS % 2
    recv_b[par, 0, :, chunk:] = dots_ref[...]
    for d in range(n - 1, 0, -1):
        send_b[par, d, :, chunk:] = dots_ref[...]
        b_copy(par, d).start()
    for d in range(1, n):
        b_copy(par, d).wait_recv()
    total = start_sums(par)
    for d in range(1, n):
        b_copy(par, d).wait_send()
    gam, dlt = end_sums(par, total)
    b = gam / gam_old
    a = gam / (dlt - b * gam / a_old)
    for i in range(rows_x):
        at = slice(i * rows_y, (i + 1) * rows_y)
        r = r_ref[at, :]
        p = r * inv_ref[at, :] + b * p_ref[at, :]
        s = w_ref[at, :] + b * s_ref[at, :]
        x_ref[at, :] = x_ref[at, :] + a * p
        r_ref[at, :] = r - a * s


def hand_on(x_ref, r_ref, x_out, r_out):
    x_out[...] = x_ref[...]
    r_out[...] = r_ref[...]


def local(
    right_side,
    accumulation,
    trans_x,
    trans_y,
    trans_z,
    perf_cells,
    perf_live,
    well_region,
    schur_blocks,
):
    rows_x, rows_y, layers = right_side.shape
    cols = rows_x * rows_y
    wells, perf = perf_cells.shape
    n, ny = lax.axis_size("gx"), lax.axis_size("gy")
    chunk = WCAP * perf
    f32, bf16, i32 = jnp.float32, jnp.bfloat16, jnp.int32
    vmem, dma = pltpu.VMEM, pltpu.SemaphoreType.DMA
    field = vmem((cols, layers), f32)
    fields = [value.reshape(cols, layers) for value in (right_side, accumulation, trans_x, trans_y, trans_z)]
    in_vmem = pl.BlockSpec(memory_space=pltpu.VMEM)
    outs = pl.pallas_call(
        functools.partial(kernel, n, ny, rows_x, rows_y),
        out_shape=[jax.ShapeDtypeStruct((cols, layers), f32)] * 2,
        in_specs=[pl.BlockSpec(memory_space=pltpu.SMEM)]
        + [pl.BlockSpec(memory_space=pl.ANY)] * 5
        + [in_vmem] * 2
        + [pl.BlockSpec(memory_space=pl.ANY)],
        out_specs=[in_vmem] * 2,
        scratch_shapes=[field] * 5
        + [
            vmem((wells, perf, perf), f32),
            vmem((n * WCAP, 2 * perf, perf), bf16),
            vmem((cols, n * chunk), bf16),
            vmem((2 * layers, n * chunk), bf16),
            vmem((n, 1, chunk), i32),
            vmem((n, 1, chunk), f32),
            vmem((n, 1, chunk), i32),
            vmem((n, 1, chunk), i32),
            vmem((2, n, 1, chunk + layers), f32),
            vmem((2, n, 1, chunk + layers), f32),
            vmem((2, n, 1, chunk), f32),
            vmem((2, n, 1, chunk), f32),
            vmem((2, 1, layers), f32),
            vmem((2, ny, 1, layers), f32),
            vmem((2, 2, rows_x, layers), f32),
            vmem((2, 2, rows_y, layers), f32),
            vmem((2, 2, rows_x, layers), f32),
            vmem((rows_x, layers), f32),
            vmem((rows_y, layers), f32),
            vmem((rows_x, layers), f32),
            vmem((cols + rows_y, layers), f32),
        ]
        + [field] * 11
        + [
            vmem((1, layers), f32),
            dma,
            dma((5,)),
            dma((n,)),
            dma((n,)),
            dma((2,)),
            dma((2,)),
            dma((2, 4)),
            dma((2, 4)),
            dma((2, n)),
            dma((2, n)),
            dma((2, n)),
            dma((2, n)),
            dma((2, ny)),
            dma((2, ny)),
        ],
        compiler_params=pltpu.CompilerParams(
            collective_id=0, has_side_effects=True, vmem_limit_bytes=60 * 1024 * 1024
        ),
    )(well_region.reshape(1, wells), *fields, perf_cells, perf_live, schur_blocks)
    outs = pl.pallas_call(
        hand_on,
        out_shape=[jax.ShapeDtypeStruct((cols, layers), f32)] * 2,
        in_specs=[in_vmem] * 2,
        out_specs=[in_vmem] * 2,
    )(*outs)
    return tuple(value.reshape(right_side.shape) for value in outs)


def solution(mesh):
    field, rows = P("gx", "gy", None), P(("gx", "gy"), None)
    return jax.shard_map(
        local,
        mesh=mesh,
        in_specs=(field,) * 5 + (rows,) * 3 + (P(("gx", "gy"), None, None),),
        out_specs=(field, field),
        check_vma=False,
    )
```
